256 devices in a mesh: section: 2 (over core), expert: 64 (over y, x, z_lo), head: 2 (over z_hi).
Axes of the slice: x: 4, y: 4, z: 8 (z_hi: 2, z_lo: 4; z = z_hi * 4 + z_lo), core: 2. Of those that a mesh axis runs over, the one named last changes fastest.
Arguments:
- boundary: bfloat16 [2, 2, 8192, 768], P('section', None, 'expert', 'head'), may hold values from -6 to 6
- norm_gain: float32 [2, 768], P('section'), may hold values from 0.25 to 1.75
- gate_prob: float32 [2, 2, 8192], P('section', None, 'expert'), may hold values from 0.25 to 1
- expert_ids: int32 [2, 2, 8192], P('section', None, 'expert'), may hold values from 0 to 63, as said below
- slot_ids: int32 [2, 2, 8192], P('section', None, 'expert'), may hold values from 0 to 4, as said below
- weight_in: bfloat16 [2, 64, 768, 3072], P('section', 'expert', None, 'head'), may hold values from -0.21875 to 0.21875
- weight_out: bfloat16 [2, 64, 3072, 768], P('section', 'expert', 'head'), may hold values from -0.109375 to 0.109375
Outputs:
- boundary_out: bfloat16 [2, 2, 8192, 768], P('section', None, 'expert', 'head')
- grad_in: bfloat16 [2, 64, 768, 3072], P('section', 'expert', None, 'head')
- grad_out: bfloat16 [2, 64, 3072, 768], P('section', 'expert', 'head')
The draws below stay inside these ranges and needn't reach their ends.
Inputs may be any that keep to these rules, and one draw needn't show every extreme that they name: `expert_ids`: within each layer and micro-batch, tokens are taken in blocks of 128 (the tokens of one index of expert); in every block one expert, the same for all blocks of that layer and micro-batch, is named by more than 4 tokens. `slot_ids`: A token's slot is the number of earlier tokens of its block that name the same expert, capped at 4; 4 means the token is dropped. So at most 4 tokens of a block hold a slot below 4 at one expert, and in every layer and micro-batch one expert has all 4 slots filled from every block.
All inputs are finite; a program needn't handle non-finite values.
Results may differ from the reference program's by a relative error of at most 0.008.
Values may be sent and summed in bfloat16 or wider, within the bound.
No kernel may reach another device: no remote copies, remote signals or barrier semaphores. Data moves between devices by JAX's collectives and lax.ppermute only.
A program may use at most 128 MiB of HBM per device.

```python
import jax
import jax.numpy as jnp
from jax import lax

D = 768
FF = 3072
TOK_DEV = 128
MICRO = 2
EXPERTS = 64
TOKENS = 8192
CAP = 4


def routing(key):
    block_count = TOKENS // TOK_DEV
    streams = jax.random.split(jax.random.fold_in(key, 11), 3)
    favored = jax.random.randint(streams[0], (2, MICRO, 1, 1), 0, EXPERTS)
    random_ids = jax.random.randint(streams[1], (2, MICRO, block_count, TOK_DEV), 0, EXPERTS)
    position = jnp.arange(TOK_DEV, dtype=jnp.int32)
    chosen = jnp.where(position < CAP + 1, favored, random_ids)
    shuffle_score = jax.random.randint(streams[2], (2, MICRO, block_count, TOK_DEV), 0, 2 ** 18) * 4096 + position
    shuffle = jnp.argsort(shuffle_score, axis=-1)
    route_ids = jnp.take_along_axis(chosen, shuffle, axis=-1)
    onehot = (route_ids[..., None] == jnp.arange(EXPERTS, dtype=jnp.int32)).astype(jnp.int32)
    earlier = jnp.sum((jnp.cumsum(onehot, axis=-2) - onehot) * onehot, axis=-1)
    slot_rank = jnp.minimum(earlier, CAP)
    return (route_ids.reshape(2, MICRO, TOKENS).astype(jnp.int32), slot_rank.reshape(2, MICRO, TOKENS).astype(jnp.int32))


def draw_expert_ids(key, part):
    return routing(key)[0]


def draw_slot_ids(key, part):
    return routing(key)[1]


def shard_levels(key, dims, shards, smallest, largest):
    def one(dim, shards_of):
        heights = jax.random.uniform(jax.random.fold_in(jax.random.fold_in(key, 6), dim), (shards_of,), jnp.float32, smallest / len(shards), largest / len(shards))
        return jnp.repeat(jnp.exp(heights), dims[dim] // shards_of).reshape((-1,) + (1,) * (len(dims) - dim - 1))

    factor_of = one(*shards[0])
    for cut in shards[1:]:
        factor_of = factor_of * one(*cut)
    return factor_of


def noise(own_key, extent, deviation, limit, cuts=(), kind=jnp.bfloat16):
    array = deviation * jax.random.normal(own_key, extent, jnp.float32)
    if cuts:
        array = array * shard_levels(own_key, extent, cuts, -0.22, 0.18)
    return jnp.clip(array, -limit, limit).astype(kind)


def setup_inputs(seed: int = 0) -> dict:
    seeds = jax.random.split(jax.random.key(seed), 8)
    boundary = noise(seeds[0], (2, MICRO, TOKENS, D), 1.0, 6.0, ((0, 2), (2, 64), (3, 2)))
    norm_gain = jnp.clip(1.0 + 0.15 * jax.random.normal(seeds[1], (2, D), jnp.float32), 0.25, 1.75)
    gate_prob = jnp.clip(0.25 + 0.75 * jax.random.uniform(seeds[2], (2, MICRO, TOKENS), jnp.float32) ** shard_levels(seeds[2], (2, MICRO, TOKENS), ((0, 2), (2, 64)), -0.2, 0.2), 0.25, 1.0)
    expert_ids = draw_expert_ids(jax.random.fold_in(seeds[7], 71), 0)
    slot_ids = draw_slot_ids(jax.random.fold_in(seeds[7], 71), 0)
    weight_in = noise(seeds[5], (2, EXPERTS, D, FF), D ** -0.5, 0.21875, ((0, 2), (1, 64), (3, 2)))
    weight_out = noise(seeds[6], (2, EXPERTS, FF, D), FF ** -0.5, 0.109375, ((0, 2), (1, 64), (2, 2)))
    return {"boundary": boundary, "norm_gain": norm_gain, "gate_prob": gate_prob, "expert_ids": expert_ids, "slot_ids": slot_ids, "weight_in": weight_in, "weight_out": weight_out}


EPSILON = 1e-06
ROOT_COEF = 0.7978845608
CUBE_COEF = 0.044715

def activate(pre_act):
    tangent = jnp.tanh(ROOT_COEF * (pre_act + CUBE_COEF * pre_act * pre_act * pre_act))
    act_value = 0.5 * pre_act * (1.0 + tangent)
    act_slope = 0.5 * (1.0 + tangent) + 0.5 * pre_act * (1.0 - tangent * tangent) * ROOT_COEF * (1.0 + 3.0 * CUBE_COEF * pre_act * pre_act)
    return (act_value, act_slope)

def rounded(values):
    return lax.optimization_barrier(values.astype(jnp.bfloat16)).astype(jnp.float32)

def placement_rows(slot_ids):
    block_of = jnp.arange(TOKENS, dtype=jnp.int32) // TOK_DEV
    kept_mask = slot_ids < CAP
    row_of = jnp.where(kept_mask, block_of * CAP + slot_ids, TOKENS // TOK_DEV * CAP).astype(jnp.int32)
    return (kept_mask, row_of)

def dispatch(tokens, expert_ids, row_of):
    buffer = jnp.zeros((EXPERTS, TOKENS // TOK_DEV * CAP, D), tokens.dtype)
    return buffer.at[expert_ids, row_of].set(tokens, mode='drop')

def collect(buffer, expert_ids, row_of, kept_mask):
    last_row = buffer.shape[1] - 1
    picked = buffer[expert_ids, jnp.minimum(row_of, last_row)]
    return jnp.where(kept_mask[:, None], picked.astype(jnp.float32), jnp.float32(0.0))

def normalize(rows_in, gain):
    values = rows_in.astype(jnp.float32)
    inv_scale = lax.rsqrt(lax.optimization_barrier(jnp.mean(values * values, axis=-1, keepdims=True)) + EPSILON)
    return (values * inv_scale * gain).astype(jnp.bfloat16)

def layer_forward(tokens, gain, weight_in, weight_out, expert_ids, slot_ids, gate_prob):
    kept_mask, row_of = placement_rows(slot_ids)
    buffer = dispatch(tokens, expert_ids, row_of)
    half_ff = FF // 2

    def per_expert(operands):
        rows_in, first_weight, second_weight = operands
        normed = normalize(rows_in, gain)
        pre_act = jnp.dot(normed, first_weight, preferred_element_type=jnp.float32)
        act_value = activate(pre_act)[0].astype(jnp.bfloat16)
        part_low = jnp.dot(act_value[:, :half_ff], second_weight[:half_ff], preferred_element_type=jnp.float32)
        part_high = jnp.dot(act_value[:, half_ff:], second_weight[half_ff:], preferred_element_type=jnp.float32)
        return (rounded(part_low) + rounded(part_high)).astype(jnp.bfloat16)
    outputs = lax.map(per_expert, (buffer, weight_in, weight_out))
    combined = collect(outputs, expert_ids, row_of, kept_mask)
    return (tokens.astype(jnp.float32) + gate_prob[:, None] * combined).astype(jnp.bfloat16)

def layer_backward(tokens, grad_tok, gain, weight_in, weight_out, expert_ids, slot_ids, gate_prob):
    kept_mask, row_of = placement_rows(slot_ids)
    buffer = dispatch(tokens, expert_ids, row_of)
    sent_grad = (gate_prob[:, None] * grad_tok.astype(jnp.float32)).astype(jnp.bfloat16)
    grad_buffer = dispatch(sent_grad, expert_ids, row_of)
    half_ff = FF // 2

    def per_expert(operands):
        rows_in, grad_rows, first_weight, second_weight = operands
        normed = normalize(rows_in, gain)
        pre_act = jnp.dot(normed, first_weight, preferred_element_type=jnp.float32)
        act_slope = activate(pre_act)[1]
        grad_act = jnp.dot(grad_rows, second_weight.T, preferred_element_type=jnp.float32)
        grad_pre = (grad_act * act_slope).astype(jnp.bfloat16)
        part_low = jnp.dot(grad_pre[:, :half_ff], first_weight[:, :half_ff].T, preferred_element_type=jnp.float32)
        part_high = jnp.dot(grad_pre[:, half_ff:], first_weight[:, half_ff:].T, preferred_element_type=jnp.float32)
        return (rounded(part_low) + rounded(part_high)).astype(jnp.bfloat16)
    grad_normed = lax.map(per_expert, (buffer, grad_buffer, weight_in, weight_out))
    grad_back = collect(grad_normed, expert_ids, row_of, kept_mask)
    values = tokens.astype(jnp.float32)
    inv_scale = lax.rsqrt(lax.optimization_barrier(jnp.mean(values * values, axis=-1, keepdims=True)) + EPSILON)
    scaled_grad = gain * grad_back
    cross_sum = lax.optimization_barrier(jnp.sum(scaled_grad * values, axis=-1, keepdims=True))
    result = grad_tok.astype(jnp.float32) + inv_scale * scaled_grad - values * inv_scale * inv_scale * inv_scale * cross_sum / D
    return result.astype(jnp.bfloat16)

def layer_gradients(inputs, cotangents, gain, weight_in, weight_out, expert_ids, slot_ids, gate_prob):
    row_buffers = []
    grad_buffers = []
    for micro_index in range(MICRO):
        kept_mask, row_of = placement_rows(slot_ids[micro_index])
        row_buffers.append(dispatch(inputs[micro_index], expert_ids[micro_index], row_of))
        sent_grad = (gate_prob[micro_index][:, None] * cotangents[micro_index].astype(jnp.float32)).astype(jnp.bfloat16)
        grad_buffers.append(dispatch(sent_grad, expert_ids[micro_index], row_of))
    rows_all = jnp.stack(row_buffers, axis=1)
    grads_all = jnp.stack(grad_buffers, axis=1)

    def per_expert(operands):
        rows_each, grads_each, first_weight, second_weight = operands
        total_in = jnp.zeros((D, FF), jnp.float32)
        total_out = jnp.zeros((FF, D), jnp.float32)
        for micro_index in range(MICRO):
            normed = normalize(rows_each[micro_index], gain)
            pre_act = jnp.dot(normed, first_weight, preferred_element_type=jnp.float32)
            act_value, act_slope = activate(pre_act)
            grad_act = jnp.dot(grads_each[micro_index], second_weight.T, preferred_element_type=jnp.float32)
            grad_pre = (grad_act * act_slope).astype(jnp.bfloat16)
            total_in = total_in + jnp.dot(normed.T, grad_pre, preferred_element_type=jnp.float32)
            total_out = total_out + jnp.dot(act_value.astype(jnp.bfloat16).T, grads_each[micro_index], preferred_element_type=jnp.float32)
        return (total_in.astype(jnp.bfloat16), total_out.astype(jnp.bfloat16))
    return lax.map(per_expert, (rows_all, grads_all, weight_in, weight_out))

def reference(boundary, norm_gain, gate_prob, expert_ids, slot_ids, weight_in, weight_out):
    hiddens = []
    tops = []
    grad_hiddens = []
    bottoms = []
    for micro_index in range(MICRO):
        hidden = layer_forward(boundary[0, micro_index], norm_gain[0], weight_in[0], weight_out[0], expert_ids[0, micro_index], slot_ids[0, micro_index], gate_prob[0, micro_index])
        top_out = layer_forward(hidden, norm_gain[1], weight_in[1], weight_out[1], expert_ids[1, micro_index], slot_ids[1, micro_index], gate_prob[1, micro_index])
        grad_hidden = layer_backward(hidden, boundary[1, micro_index], norm_gain[1], weight_in[1], weight_out[1], expert_ids[1, micro_index], slot_ids[1, micro_index], gate_prob[1, micro_index])
        bottom = layer_backward(boundary[0, micro_index], grad_hidden, norm_gain[0], weight_in[0], weight_out[0], expert_ids[0, micro_index], slot_ids[0, micro_index], gate_prob[0, micro_index])
        hiddens.append(hidden)
        tops.append(top_out)
        grad_hiddens.append(grad_hidden)
        bottoms.append(bottom)
    boundary_out = jnp.stack([jnp.stack(bottoms), jnp.stack(tops)])
    lower_in, lower_out = layer_gradients(boundary[0], jnp.stack(grad_hiddens), norm_gain[0], weight_in[0], weight_out[0], expert_ids[0], slot_ids[0], gate_prob[0])
    upper_in, upper_out = layer_gradients(jnp.stack(hiddens), boundary[1], norm_gain[1], weight_in[1], weight_out[1], expert_ids[1], slot_ids[1], gate_prob[1])
    return (boundary_out, jnp.stack([lower_in, upper_in]), jnp.stack([lower_out, upper_out]))
```

```python
import functools

import jax
import jax.numpy as jnp
from jax import lax
from jax.experimental import pallas as pl
from jax.experimental.pallas import tpu as pltpu
from jax.sharding import PartitionSpec as P

EPSILON = 1e-06
ROOT_COEF = 0.7978845608
CUBE_COEF = 0.044715
VMEM_LIMIT = 40 * 1024 * 1024
BF16, F32 = jnp.bfloat16, jnp.float32


def activate(v):
    sq = v * v
    th = jnp.tanh(ROOT_COEF * (v + CUBE_COEF * sq * v))
    up = 0.5 * (1.0 + th)
    return th, sq, up


def act_of(v):
    _, _, up = activate(v)
    return v * up


def act_and_slope(v):
    th, sq, up = activate(v)
    slope = up + 0.5 * v * (1.0 - th * th) * (ROOT_COEF + (3.0 * CUBE_COEF * ROOT_COEF) * sq)
    return v * up, slope


def dot(a, b, dims=((1,), (0,))):
    return lax.dot_general(a, b, (dims, ((), ())), preferred_element_type=F32)


def call(body, outs, ins, flops, grid=(), in_specs=None, out_specs=None, scratch=(), name=None):
    moved = sum(a.size * a.dtype.itemsize for a in ins)
    moved += sum(s.size * s.dtype.itemsize for s in outs)
    kwargs = {}
    if grid:
        kwargs = dict(grid=grid, in_specs=in_specs, out_specs=out_specs)
    return pl.pallas_call(
        body,
        out_shape=outs,
        scratch_shapes=scratch,
        compiler_params=pltpu.CompilerParams(vmem_limit_bytes=VMEM_LIMIT),
        cost_estimate=pl.CostEstimate(flops=flops, bytes_accessed=moved, transcendentals=0),
        name=name,
        **kwargs,
    )(*ins)


def struct(shape, dtype):
    return jax.ShapeDtypeStruct(shape, dtype)


def one_hot(ids, slots, experts, cap):
    micro, tokens = ids.shape
    per = micro * cap
    target = jnp.where(slots < cap, ids * per + slots, -1 - cap * micro)
    pieces = [target[m : m + 1] + m * cap for m in range(micro)]
    target = jnp.concatenate(pieces, axis=1)
    rows = lax.broadcasted_iota(jnp.int32, (experts * per, micro * tokens), 0)
    return (rows == target).astype(F32).astype(BF16)


def column(rows):
    flat = jnp.concatenate([rows[m : m + 1] for m in range(rows.shape[0])], axis=1)
    return jnp.transpose(jnp.broadcast_to(flat, (8, flat.shape[1])))[:, :1]


def place_body(scaled, cap, *refs):
    if scaled:
        tok, ids, slots, prob, out = refs
    else:
        tok, ids, slots, out = refs
    experts, heads, per, half = out.shape
    tokens = tok[...].reshape(-1, half)
    if scaled:
        tokens = (column(prob[...]) * tokens.astype(F32)).astype(BF16)
    hot = one_hot(ids[...], slots[...], experts, cap)
    rows = dot(hot, tokens).reshape(experts, per, half).astype(BF16)
    for h in range(heads):
        out[:, h] = rows


def place(tokens, ids, slots, prob, experts, cap):
    micro, count, half = tokens.shape
    out = struct((experts, 2, micro * cap, half), BF16)
    ins = (tokens, ids, slots) + (() if prob is None else (prob,))
    flops = 2 * experts * micro * cap * micro * count * half
    return call(functools.partial(place_body, prob is not None, cap), [out], ins, flops, name="place")[0]


def gather_body(forward, cap, *refs):
    if forward:
        got, ids, slots, prob, base, out = refs
    else:
        got, ids, slots, base, out = refs
    experts, heads, per, half = got.shape
    hot = one_hot(ids[...], slots[...], experts, cap)
    first = got[:, 0].astype(F32).reshape(experts * per, half)
    second = got[:, 1].astype(F32).reshape(experts * per, half)
    if forward:
        picked = dot(hot, (first + second).astype(BF16), ((0,), (0,)))
        picked = column(prob[...]) * picked
    else:
        picked = dot(hot, first.astype(BF16), ((0,), (0,))) + dot(hot, second.astype(BF16), ((0,), (0,)))
    total = base[...].reshape(-1, half).astype(F32) + picked
    out[...] = total.astype(BF16).reshape(out.shape)


def gather(got, ids, slots, prob, base, cap):
    ins = (got, ids, slots) + (() if prob is None else (prob,)) + (base,)
    flops = 2 * got.shape[0] * got.shape[2] * base.size
    return call(
        functools.partial(gather_body, prob is not None, cap), [struct(base.shape, BF16)], ins, flops, name="gather"
    )[0]


def rows_of(ref):
    experts, heads, per, half = ref.shape
    return [ref[:, h].astype(F32).reshape(experts * per, half) for h in range(heads)]


def inverse(parts, width):
    total = sum(jnp.sum(v * v, axis=1, keepdims=True) for v in parts)
    return lax.rsqrt(total * (1.0 / width) + EPSILON)


def fill_normed(rows_ref, gain_ref, normed_ref):
    parts = rows_of(rows_ref)
    half = parts[0].shape[1]
    scale = inverse(parts, 2 * half)
    for h, v in enumerate(parts):
        cols = pl.ds(h * half, half)
        normed_ref[:, cols] = (v * scale * gain_ref[:, cols]).astype(BF16)


def spread(total_ref, out_ref):
    experts, heads, per, half = out_ref.shape
    for h in range(heads):
        piece = total_ref[:, pl.ds(h * half, half)]
        out_ref[:, h] = piece.reshape(experts, per, half).astype(BF16)


def spread_norm_grad(total_ref, rows_ref, gain_ref, out_ref):
    experts, heads, per, half = out_ref.shape
    parts = rows_of(rows_ref)
    scale = inverse(parts, heads * half)
    grads = [total_ref[:, pl.ds(h * half, half)] * gain_ref[:, pl.ds(h * half, half)] for h in range(heads)]
    cross = sum(jnp.sum(g * v, axis=1, keepdims=True) for g, v in zip(grads, parts))
    factor = scale * scale * scale * cross * (1.0 / (heads * half))
    for h in range(heads):
        piece = scale * grads[h] - parts[h] * factor
        out_ref[:, h] = piece.reshape(experts, per, half).astype(BF16)


def forward_body(rows, gain, w_in, w_out, out, pre_out, act_out, normed, total):
    step = pl.program_id(0)

    @pl.when(step == 0)
    def _():
        fill_normed(rows, gain, normed)

    pre = dot(normed[...], w_in[...])
    pre_out[...] = pre
    act = act_of(pre).astype(BF16)
    act_out[...] = act
    part = dot(act, w_out[...])

    @pl.when(step == 0)
    def _():
        total[...] = part

    @pl.when(step > 0)
    def _():
        total[...] += part

    @pl.when(step == pl.num_programs(0) - 1)
    def _():
        spread(total, out)


def whole(shape):
    return pl.BlockSpec(shape, lambda j: (0,) * len(shape))


CHUNK = 512


def sizes(rows, w_in):
    count = rows.shape[0] * rows.shape[2]
    width, hidden = w_in.shape
    return count, width, hidden


def expert_forward(rows, gain, w_in, w_out):
    count, width, hidden = sizes(rows, w_in)
    chunk = CHUNK
    cols = pl.BlockSpec((count, chunk), lambda j: (0, j))
    return call(
        forward_body,
        [
            struct(rows.shape, BF16),
            struct((count, hidden), F32),
            struct((count, hidden), BF16),
            struct((count, width), BF16),
        ],
        (rows, gain, w_in, w_out),
        4 * count * width * hidden,
        grid=(hidden // chunk,),
        in_specs=[
            whole(rows.shape),
            whole(gain.shape),
            pl.BlockSpec((width, chunk), lambda j: (0, j)),
            pl.BlockSpec((chunk, width), lambda j: (j, 0)),
        ],
        out_specs=[whole(rows.shape), cols, cols, whole((count, width))],
        scratch=[pltpu.VMEM((count, width), F32)],
        name="expert_forward",
    )


def grad_act_body(grads, w_out, out, flat):
    @pl.when(pl.program_id(0) == 0)
    def _():
        half = grads.shape[3]
        for h, v in enumerate(rows_of(grads)):
            flat[:, pl.ds(h * half, half)] = v.astype(BF16)

    out[...] = dot(flat[...], w_out[...], ((1,), (1,)))


def grad_act_early(grads, w_out):
    hidden, width = w_out.shape
    count = grads.shape[0] * grads.shape[2]
    chunk = CHUNK
    return call(
        grad_act_body,
        [struct((count, hidden), F32), struct((count, width), BF16)],
        (grads, w_out),
        2 * count * width * hidden,
        grid=(hidden // chunk,),
        in_specs=[whole(grads.shape), pl.BlockSpec((chunk, width), lambda j: (j, 0))],
        out_specs=[pl.BlockSpec((count, chunk), lambda j: (0, j)), whole((count, width))],
        name="grad_act",
    )


def both_body(rows, gain, w_in, grad_act, out, act_out, pre_grad_out, normed, total):
    step = pl.program_id(0)

    @pl.when(step == 0)
    def _():
        fill_normed(rows, gain, normed)

    weight = w_in[...]
    act, slope = act_and_slope(dot(normed[...], weight))
    act_out[...] = act.astype(BF16)
    pre_grad = (grad_act[...] * slope).astype(BF16)
    pre_grad_out[...] = pre_grad
    part = dot(pre_grad, weight, ((1,), (1,)))

    @pl.when(step == 0)
    def _():
        total[...] = part

    @pl.when(step > 0)
    def _():
        total[...] += part

    @pl.when(step == pl.num_programs(0) - 1)
    def _():
        spread_norm_grad(total, rows, gain, out)


def expert_both(rows, gain, w_in, grad_act):
    count, width, hidden = sizes(rows, w_in)
    chunk = CHUNK
    cols = pl.BlockSpec((count, chunk), lambda j: (0, j))
    return call(
        both_body,
        [
            struct(rows.shape, BF16),
            struct((count, hidden), BF16),
            struct((count, hidden), BF16),
            struct((count, width), BF16),
        ],
        (rows, gain, w_in, grad_act),
        4 * count * width * hidden,
        grid=(hidden // chunk,),
        in_specs=[
            whole(rows.shape),
            whole(gain.shape),
            pl.BlockSpec((width, chunk), lambda j: (0, j)),
            cols,
        ],
        out_specs=[whole(rows.shape), cols, cols, whole((count, width))],
        scratch=[pltpu.VMEM((count, width), F32)],
        name="expert_both",
    )


def out_body(act, w_out, out, total):
    step = pl.program_id(0)
    part = dot(act[...], w_out[...])

    @pl.when(step == 0)
    def _():
        total[...] = part

    @pl.when(step > 0)
    def _():
        total[...] += part

    @pl.when(step == pl.num_programs(0) - 1)
    def _():
        spread(total, out)


def expert_out(act, w_out, shape):
    count, hidden = act.shape
    width = w_out.shape[1]
    chunk = CHUNK
    return call(
        out_body,
        [struct(shape, BF16)],
        (act, w_out),
        2 * count * width * hidden,
        grid=(hidden // chunk,),
        in_specs=[
            pl.BlockSpec((count, chunk), lambda j: (0, j)),
            pl.BlockSpec((chunk, width), lambda j: (j, 0)),
        ],
        out_specs=[whole(shape)],
        scratch=[pltpu.VMEM((count, width), F32)],
        name="expert_out",
    )[0]


def backward_body(grads, slope, w_in, w_out, rows, gain, out, pre_grad_out, flat, total):
    step = pl.program_id(0)

    @pl.when(step == 0)
    def _():
        half = grads.shape[3]
        for h, v in enumerate(rows_of(grads)):
            flat[:, pl.ds(h * half, half)] = v.astype(BF16)

    grad_act = dot(flat[...], w_out[...], ((1,), (1,)))
    pre_grad = (grad_act * slope[...]).astype(BF16)
    pre_grad_out[...] = pre_grad
    part = dot(pre_grad, w_in[...], ((1,), (1,)))

    @pl.when(step == 0)
    def _():
        total[...] = part

    @pl.when(step > 0)
    def _():
        total[...] += part

    @pl.when(step == pl.num_programs(0) - 1)
    def _():
        spread_norm_grad(total, rows, gain, out)


def expert_backward(grads, slope, w_in, w_out, rows, gain):
    count, width, hidden = sizes(rows, w_in)
    chunk = CHUNK
    cols = pl.BlockSpec((count, chunk), lambda j: (0, j))
    return call(
        backward_body,
        [struct(rows.shape, BF16), struct((count, hidden), BF16), struct((count, width), BF16)],
        (grads, slope, w_in, w_out, rows, gain),
        4 * count * width * hidden,
        grid=(hidden // chunk,),
        in_specs=[
            whole(grads.shape),
            cols,
            pl.BlockSpec((width, chunk), lambda j: (0, j)),
            pl.BlockSpec((chunk, width), lambda j: (j, 0)),
            whole(rows.shape),
            whole(gain.shape),
        ],
        out_specs=[whole(rows.shape), cols, whole((count, width))],
        scratch=[pltpu.VMEM((count, width), F32)],
        name="expert_backward",
    )


def weight_grad_body(normed, pre_grad, act, flat, first, second):
    first[...] = dot(normed[...], pre_grad[...], ((0,), (0,))).astype(BF16)
    second[...] = dot(act[...], flat[...], ((0,), (0,))).astype(BF16)


def weight_grads(normed, pre_grad, act, flat):
    count, width = normed.shape
    hidden = act.shape[1]
    chunk = CHUNK
    cols = pl.BlockSpec((count, chunk), lambda j: (0, j))
    return call(
        weight_grad_body,
        [struct((width, hidden), BF16), struct((hidden, width), BF16)],
        (normed, pre_grad, act, flat),
        4 * count * width * hidden,
        grid=(hidden // chunk,),
        in_specs=[whole(normed.shape), cols, cols, whole(flat.shape)],
        out_specs=[
            pl.BlockSpec((width, chunk), lambda j: (0, j)),
            pl.BlockSpec((chunk, width), lambda j: (j, 0)),
        ],
        name="weight_grads",
    )


def exchange(blocks):
    experts, heads, per, half = blocks.shape
    flat = blocks.reshape(experts * heads, per, half)
    return lax.all_to_all(flat, ("expert", "head"), 0, 0, tiled=True).reshape(blocks.shape)


def swap(block):
    count = lax.axis_size("section")
    return lax.ppermute(block, "section", [(i, (i + 1) % count) for i in range(count)])


def on_device(boundary, norm_gain, gate_prob, expert_ids, slot_ids, weight_in, weight_out):
    experts = lax.axis_size("expert")
    local = boundary[0]
    micro, count, half = local.shape
    cap = 2 * count // experts
    w_in = weight_in[0, 0]
    w_out = weight_out[0, 0]
    width, hidden = w_in.shape
    ids, slots, prob = expert_ids[0], slot_ids[0], gate_prob[0]
    rows_shape = (experts, 2, micro * cap, half)
    rows_count = experts * micro * cap
    first = lax.axis_index("section") == 0

    def stage_one_lower():
        rows = exchange(place(local, ids, slots, None, experts, cap))
        part, pre, act, normed = expert_forward(rows, norm_gain, w_in, w_out)
        hid = gather(exchange(part), ids, slots, prob, local, cap)
        return hid, rows, pre, act, normed

    def stage_one_upper():
        grads = exchange(place(local, ids, slots, prob, experts, cap))
        grad_act, flat = grad_act_early(grads, w_out)
        return local, grads, grad_act, jnp.zeros((rows_count, hidden), BF16), flat

    sent, rows_one, wide, act_one, flat_one = lax.cond(first, stage_one_lower, stage_one_upper)
    hid = swap(sent)

    def stage_two_lower():
        slope = act_and_slope(wide)[1]
        return local, slope, rows_one, act_one, jnp.zeros((rows_count, hidden), BF16), flat_one

    def stage_two_upper():
        rows = exchange(place(hid, ids, slots, None, experts, cap))
        back, act, pre_grad, normed = expert_both(rows, norm_gain, w_in, wide)
        got = exchange(back)
        part = expert_out(act, w_out, rows_shape)
        grad_hid = gather(got, ids, slots, None, local, cap)
        return grad_hid, wide, part, act, pre_grad, normed

    sent, slope, part, act, pre_grad, normed = lax.cond(first, stage_two_lower, stage_two_upper)
    grad_hid = swap(sent)

    def stage_three_lower():
        grads = exchange(place(grad_hid, ids, slots, prob, experts, cap))
        back, pre_grad_low, flat = expert_backward(grads, slope, w_in, w_out, part, norm_gain)
        got = exchange(back)
        first_grad, second_grad = weight_grads(normed, pre_grad_low, act, flat)
        result = gather(got, ids, slots, None, grad_hid, cap)
        return result, first_grad, second_grad

    def stage_three_upper():
        got = exchange(part)
        first_grad, second_grad = weight_grads(normed, pre_grad, act, flat_one)
        result = gather(got, ids, slots, prob, hid, cap)
        return result, first_grad, second_grad

    result, first_grad, second_grad = lax.cond(first, stage_three_lower, stage_three_upper)
    return result[None], first_grad[None, None], second_grad[None, None]


def solution(mesh):
    placed = (
        P("section", None, "expert", "head"),
        P("section", None),
        P("section", None, "expert"),
        P("section", None, "expert"),
        P("section", None, "expert"),
        P("section", "expert", None, "head"),
        P("section", "expert", "head", None),
    )
    return jax.shard_map(
        on_device,
        mesh=mesh,
        in_specs=placed,
        out_specs=(
            P("section", None, "expert", "head"),
            P("section", "expert", None, "head"),
            P("section", "expert", "head", None),
        ),
        check_vma=False,
    )
```

```python
import functools

import jax
import jax.numpy as jnp
from jax import lax
from jax.experimental import pallas as pl
from jax.experimental.pallas import tpu as pltpu
from jax.sharding import PartitionSpec as P

EPSILON = 1e-06
ROOT_COEF = 0.7978845608
CUBE_COEF = 0.044715
VMEM_LIMIT = 40 * 1024 * 1024
BF16, F32 = jnp.bfloat16, jnp.float32


def activate(v):
    sq = v * v
    th = jnp.tanh(ROOT_COEF * (v + CUBE_COEF * sq * v))
    up = 0.5 * (1.0 + th)
    return th, sq, up


def act_of(v):
    _, _, up = activate(v)
    return v * up


def act_and_slope(v):
    th, sq, up = activate(v)
    slope = up + 0.5 * v * (1.0 - th * th) * (ROOT_COEF + (3.0 * CUBE_COEF * ROOT_COEF) * sq)
    return v * up, slope


def dot(a, b, dims=((1,), (0,))):
    return lax.dot_general(a, b, (dims, ((), ())), preferred_element_type=F32)


def call(body, outs, ins, flops, grid=(), in_specs=None, out_specs=None, scratch=(), name=None):
    moved = sum(a.size * a.dtype.itemsize for a in ins)
    moved += sum(s.size * s.dtype.itemsize for s in outs)
    kwargs = {}
    if grid:
        kwargs = dict(grid=grid, in_specs=in_specs, out_specs=out_specs)
    return pl.pallas_call(
        body,
        out_shape=outs,
        scratch_shapes=scratch,
        compiler_params=pltpu.CompilerParams(vmem_limit_bytes=VMEM_LIMIT),
        cost_estimate=pl.CostEstimate(flops=flops, bytes_accessed=moved, transcendentals=0),
        name=name,
        **kwargs,
    )(*ins)


def struct(shape, dtype):
    return jax.ShapeDtypeStruct(shape, dtype)


def one_hot(ids, slots, experts, cap):
    micro, tokens = ids.shape
    per = micro * cap
    target = jnp.where(slots < cap, ids * per + slots, -1 - cap * micro)
    pieces = [target[m : m + 1] + m * cap for m in range(micro)]
    target = jnp.concatenate(pieces, axis=1)
    rows = lax.broadcasted_iota(jnp.int32, (experts * per, micro * tokens), 0)
    return (rows == target).astype(F32).astype(BF16)


def column(rows):
    flat = jnp.concatenate([rows[m : m + 1] for m in range(rows.shape[0])], axis=1)
    return jnp.transpose(jnp.broadcast_to(flat, (8, flat.shape[1])))[:, :1]


def place_body(scaled, cap, *refs):
    tok, ids, slots = refs[:3]
    outs = refs[4:] if scaled else refs[3:]
    prob = refs[3]
    experts, heads, per, _ = outs[0].shape
    tokens = tok[...].reshape(-1, tok.shape[2])
    if scaled:
        tokens = (column(prob[...]) * tokens.astype(F32)).astype(BF16)
    hot = one_hot(ids[...], slots[...], experts, cap)
    start = 0
    for out in outs:
        stop = start + out.shape[3]
        rows = dot(hot, tokens[:, start:stop]).reshape(experts, per, stop - start).astype(BF16)
        for h in range(heads):
            out[:, h] = rows
        start = stop


def place(tokens, ids, slots, prob, experts, cap, parts=None):
    micro, count, half = tokens.shape
    outs = [struct((experts, 2, micro * cap, part), BF16) for part in parts or (half,)]
    ins = (tokens, ids, slots) + (() if prob is None else (prob,))
    flops = 2 * experts * micro * cap * micro * count * half
    placed = call(functools.partial(place_body, prob is not None, cap), outs, ins, flops, name="place")
    return placed if parts else placed[0]


def gather_body(forward, cap, *refs):
    if forward:
        got, ids, slots, prob, base, out = refs
    else:
        got, ids, slots, base, out = refs
    experts, heads, per, half = got.shape
    hot = one_hot(ids[...], slots[...], experts, cap)
    first = got[:, 0].astype(F32).reshape(experts * per, half)
    second = got[:, 1].astype(F32).reshape(experts * per, half)
    if forward:
        picked = dot(hot, (first + second).astype(BF16), ((0,), (0,)))
        picked = column(prob[...]) * picked
    else:
        picked = dot(hot, first.astype(BF16), ((0,), (0,))) + dot(hot, second.astype(BF16), ((0,), (0,)))
    total = base[...].reshape(-1, half).astype(F32) + picked
    out[...] = total.astype(BF16).reshape(out.shape)


def gather(got, ids, slots, prob, base, cap):
    ins = (got, ids, slots) + (() if prob is None else (prob,)) + (base,)
    flops = 2 * got.shape[0] * got.shape[2] * base.size
    return call(
        functools.partial(gather_body, prob is not None, cap), [struct(base.shape, BF16)], ins, flops, name="gather"
    )[0]


def rows_of(ref):
    experts, heads, per, half = ref.shape
    return [ref[:, h].astype(F32).reshape(experts * per, half) for h in range(heads)]


def inverse(parts, width):
    total = sum(jnp.sum(v * v, axis=1, keepdims=True) for v in parts)
    return lax.rsqrt(total * (1.0 / width) + EPSILON)


def fill_normed(rows_ref, gain_ref, normed_ref):
    parts = rows_of(rows_ref)
    half = parts[0].shape[1]
    scale = inverse(parts, 2 * half)
    for h, v in enumerate(parts):
        cols = pl.ds(h * half, half)
        normed_ref[:, cols] = (v * scale * gain_ref[:, cols]).astype(BF16)


def spread(total, out_ref):
    experts, heads, per, half = out_ref.shape
    for h in range(heads):
        piece = total[:, h * half : (h + 1) * half]
        out_ref[:, h] = piece.reshape(experts, per, half).astype(BF16)


def spread_norm_grad(total, rows_ref, gain_ref, out_ref):
    experts, heads, per, half = out_ref.shape
    parts = rows_of(rows_ref)
    scale = inverse(parts, heads * half)
    grads = [total[:, h * half : (h + 1) * half] * gain_ref[:, pl.ds(h * half, half)] for h in range(heads)]
    cross = sum(jnp.sum(g * v, axis=1, keepdims=True) for g, v in zip(grads, parts))
    factor = scale * scale * scale * cross * (1.0 / (heads * half))
    for h in range(heads):
        piece = scale * grads[h] - parts[h] * factor
        out_ref[:, h] = piece.reshape(experts, per, half).astype(BF16)


def whole(shape):
    return pl.BlockSpec(shape, lambda j: (0,) * len(shape))


CHUNK = 256
GROUPS = 2


def sizes(rows, w_in):
    count = rows.shape[0] * rows.shape[2]
    width, hidden = w_in.shape
    return count, width, hidden


def expert_group(ref, r):
    step = ref.shape[0] // GROUPS
    return ref.at[pl.ds(r * step, step)]


def row_group(ref, r):
    step = ref.shape[0] // GROUPS
    return ref.at[pl.ds(pl.multiple_of(r * step, step), step)]


def over_groups(body):
    pl.loop(0, GROUPS)(body)


def copies_of(pairs, sems):
    return [pltpu.make_async_copy(src, dst, sems.at[i]) for i, (src, dst) in enumerate(pairs)]


def start_all(copies):
    for copy in copies:
        copy.start()


def flatten(grads, flat):
    half = grads.shape[3]
    for h, v in enumerate(rows_of(grads)):
        flat[:, pl.ds(h * half, half)] = v.astype(BF16)


def owned(body, outs, ins, flops, scratch, sems, name):
    moved = sum(a.size * a.dtype.itemsize for a in ins)
    moved += sum(s.size * s.dtype.itemsize for s in outs)
    return pl.pallas_call(
        body,
        out_shape=outs,
        in_specs=[
            pl.BlockSpec(memory_space=pltpu.VMEM if a.size < 4096 else pl.ANY) for a in ins
        ],
        out_specs=[pl.BlockSpec(memory_space=pl.ANY) for _ in outs],
        scratch_shapes=[pltpu.VMEM(shape, dtype) for shape, dtype in scratch] + [pltpu.SemaphoreType.DMA((sems,))],
        compiler_params=pltpu.CompilerParams(vmem_limit_bytes=VMEM_LIMIT),
        cost_estimate=pl.CostEstimate(flops=flops, bytes_accessed=moved, transcendentals=0),
        name=name,
    )(*ins)


def forward_body(rows, gain, w_in, w_out, out, rows_v, w_in_v, w_out_v, normed, out_v, sems):
    loads = copies_of([(rows, rows_v), (w_in, w_in_v), (w_out, w_out_v)], sems)
    start_all(loads)

    def stored(r):
        return pltpu.make_async_copy(expert_group(out_v, r), expert_group(out, r), sems.at[3 + r])

    loads[0].wait()

    @over_groups
    def _(r):
        fill_normed(expert_group(rows_v, r), gain, normed)

        @pl.when(r == 0)
        def _():
            loads[1].wait()

        act = act_of(dot(normed[...], w_in_v[...])).astype(BF16)

        @pl.when(r == 0)
        def _():
            loads[2].wait()

        spread(dot(act, w_out_v[...]), expert_group(out_v, r))
        stored(r).start()

    for r in range(GROUPS):
        stored(r).wait()


def expert_forward(rows, gain, w_in, w_out):
    count, width, hidden = sizes(rows, w_in)
    return owned(
        forward_body,
        [struct(rows.shape, BF16)],
        (rows, gain, w_in, w_out),
        4 * count * width * hidden,
        [
            (rows.shape, BF16),
            (w_in.shape, BF16),
            (w_out.shape, BF16),
            ((count // GROUPS, width), BF16),
            (rows.shape, BF16),
        ],
        3 + GROUPS,
        "expert_forward",
    )[0]


def grad_act_body(grads, w_out, out, flat):
    @pl.when(pl.program_id(0) == 0)
    def _():
        flatten(grads, flat)

    out[...] = dot(flat[...], w_out[...], ((1,), (1,)))


def grad_act_early(grads, w_out):
    hidden, width = w_out.shape
    count = grads.shape[0] * grads.shape[2]
    return call(
        grad_act_body,
        [struct((count, hidden), F32)],
        (grads, w_out),
        2 * count * width * hidden,
        grid=(hidden // CHUNK,),
        in_specs=[whole(grads.shape), pl.BlockSpec((CHUNK, width), lambda j: (j, 0))],
        out_specs=[pl.BlockSpec((count, CHUNK), lambda j: (0, j))],
        scratch=[pltpu.VMEM((count, width), BF16)],
        name="grad_act",
    )[0]


def slope_body(rows, gain, w_in, out, normed):
    @pl.when(pl.program_id(0) == 0)
    def _():
        fill_normed(rows, gain, normed)

    out[...] = act_and_slope(dot(normed[...], w_in[...]))[1]


def slope_of_rows(rows, gain, w_in):
    count, width, hidden = sizes(rows, w_in)
    return call(
        slope_body,
        [struct((count, hidden), F32)],
        (rows, gain, w_in),
        2 * count * width * hidden,
        grid=(hidden // CHUNK,),
        in_specs=[whole(rows.shape), whole(gain.shape), pl.BlockSpec((width, CHUNK), lambda j: (0, j))],
        out_specs=[pl.BlockSpec((count, CHUNK), lambda j: (0, j))],
        scratch=[pltpu.VMEM((count, width), BF16)],
        name="slope",
    )[0]


def both_body(rows, gain, w_in, grad_act, out, kept, rows_v, w_in_v, ga_v, normed, pre_grad, out_v, sems):
    loads = copies_of([(rows, rows_v), (w_in, w_in_v), (grad_act, ga_v)], sems)
    start_all(loads)

    def stored(r):
        return pltpu.make_async_copy(expert_group(out_v, r), expert_group(out, r), sems.at[3 + r])

    def saved(r):
        return pltpu.make_async_copy(row_group(pre_grad, r), row_group(kept, r), sems.at[3 + GROUPS + r])

    loads[0].wait()

    @over_groups
    def _(r):
        row = expert_group(rows_v, r)
        fill_normed(row, gain, normed)

        @pl.when(r == 0)
        def _():
            loads[1].wait()

        slope = act_and_slope(dot(normed[...], w_in_v[...]))[1]

        @pl.when(r == 0)
        def _():
            loads[2].wait()

        pre = (row_group(ga_v, r)[...] * slope).astype(BF16)
        row_group(pre_grad, r)[...] = pre
        saved(r).start()
        spread_norm_grad(dot(pre, w_in_v[...], ((1,), (1,))), row, gain, expert_group(out_v, r))
        stored(r).start()

    for r in range(GROUPS):
        stored(r).wait()
        saved(r).wait()


def expert_both(rows, gain, w_in, grad_act):
    count, width, hidden = sizes(rows, w_in)
    return owned(
        both_body,
        [struct(rows.shape, BF16), struct((count, hidden), BF16)],
        (rows, gain, w_in, grad_act),
        4 * count * width * hidden,
        [
            (rows.shape, BF16),
            (w_in.shape, BF16),
            ((count, hidden), F32),
            ((count // GROUPS, width), BF16),
            ((count, hidden), BF16),
            (rows.shape, BF16),
        ],
        3 + 2 * GROUPS,
        "expert_both",
    )


def backward_body(
    grads, slope, w_in, w_out, rows, gain, out, kept, grads_v, slope_v, w_in_v, w_out_v, rows_v, flat, pre_grad, out_v, sems
):
    pairs = [(grads, grads_v), (w_out, w_out_v), (slope, slope_v), (w_in, w_in_v), (rows, rows_v)]
    loads = copies_of(pairs, sems)
    start_all(loads)

    def stored(r):
        return pltpu.make_async_copy(expert_group(out_v, r), expert_group(out, r), sems.at[5 + r])

    def saved(r):
        return pltpu.make_async_copy(row_group(pre_grad, r), row_group(kept, r), sems.at[5 + GROUPS + r])

    loads[0].wait()

    @over_groups
    def _(r):
        flatten(expert_group(grads_v, r), flat)

        @pl.when(r == 0)
        def _():
            loads[1].wait()

        grad_act = dot(flat[...], w_out_v[...], ((1,), (1,)))

        @pl.when(r == 0)
        def _():
            loads[2].wait()

        pre = (grad_act * row_group(slope_v, r)[...]).astype(BF16)
        row_group(pre_grad, r)[...] = pre
        saved(r).start()

        @pl.when(r == 0)
        def _():
            loads[3].wait()
            loads[4].wait()

        total = dot(pre, w_in_v[...], ((1,), (1,)))
        spread_norm_grad(total, expert_group(rows_v, r), gain, expert_group(out_v, r))
        stored(r).start()

    for r in range(GROUPS):
        stored(r).wait()
        saved(r).wait()


def expert_backward(grads, slope, w_in, w_out, rows, gain):
    count, width, hidden = sizes(rows, w_in)
    return owned(
        backward_body,
        [struct(rows.shape, BF16), struct((count, hidden), BF16)],
        (grads, slope, w_in, w_out, rows, gain),
        4 * count * width * hidden,
        [
            (grads.shape, BF16),
            (slope.shape, F32),
            (w_in.shape, BF16),
            (w_out.shape, BF16),
            (rows.shape, BF16),
            ((count // GROUPS, width), BF16),
            ((count, hidden), BF16),
            (rows.shape, BF16),
        ],
        5 + 2 * GROUPS,
        "expert_backward",
    )


def weight_grad_body(rows, gain, grads, w_in, pre_grad, first, second, normed, flat):
    @pl.when(pl.program_id(0) == 0)
    def _():
        fill_normed(rows, gain, normed)
        flatten(grads, flat)

    first[...] = dot(normed[...], pre_grad[...], ((0,), (0,))).astype(BF16)
    act = act_of(dot(normed[...], w_in[...])).astype(BF16)
    second[...] = dot(act, flat[...], ((0,), (0,))).astype(BF16)


def weight_grads(rows, gain, grads, w_in, pre_grad):
    count, width, hidden = sizes(rows, w_in)
    columns = pl.BlockSpec((width, CHUNK), lambda j: (0, j))
    return call(
        weight_grad_body,
        [struct((width, hidden), BF16), struct((hidden, width), BF16)],
        (rows, gain, grads, w_in, pre_grad),
        6 * count * width * hidden,
        grid=(hidden // CHUNK,),
        in_specs=[
            whole(rows.shape),
            whole(gain.shape),
            whole(grads.shape),
            columns,
            pl.BlockSpec((count, CHUNK), lambda j: (0, j)),
        ],
        out_specs=[columns, pl.BlockSpec((CHUNK, width), lambda j: (j, 0))],
        scratch=[pltpu.VMEM((count, width), BF16), pltpu.VMEM((count, width), BF16)],
        name="weight_grads",
    )


def exchange(blocks):
    experts, heads, per, part = blocks.shape
    flat = blocks.reshape(experts * heads, per, part)
    return lax.all_to_all(flat, ("expert", "head"), 0, 0, tiled=True).reshape(blocks.shape)


def swap(block):
    count = lax.axis_size("section")
    return lax.ppermute(block, "section", [(i, (i + 1) % count) for i in range(count)])


def on_device(boundary, norm_gain, gate_prob, expert_ids, slot_ids, weight_in, weight_out):
    experts = lax.axis_size("expert")
    local = boundary[0]
    micro, count, half = local.shape
    cap = 2 * count // experts
    w_in = weight_in[0, 0]
    w_out = weight_out[0, 0]
    ids, slots, prob = expert_ids[0], slot_ids[0], gate_prob[0]
    first = lax.axis_index("section") == 0

    def stage_one_lower():
        rows = exchange(place(local, ids, slots, None, experts, cap))
        part = expert_forward(rows, norm_gain, w_in, w_out)
        return gather(exchange(part), ids, slots, prob, local, cap), rows

    def stage_one_upper():
        small, large = place(local, ids, slots, prob, experts, cap, (half // 3, half - half // 3))
        small, large = lax.optimization_barrier((exchange(small), large))
        return local, jnp.concatenate([small, exchange(large)], axis=3)

    sent, rows_one = lax.cond(first, stage_one_lower, stage_one_upper)
    hid = swap(sent)

    def stage_two_lower():
        slope = slope_of_rows(rows_one, norm_gain, w_in)
        return local, slope, rows_one, jnp.zeros(slope.shape, BF16)

    def stage_two_upper():
        rows = exchange(place(hid, ids, slots, None, experts, cap))
        grad_act = grad_act_early(rows_one, w_out)
        back, pre_grad = expert_both(rows, norm_gain, w_in, grad_act)
        grad_hid = gather(exchange(back), ids, slots, None, local, cap)
        return grad_hid, grad_act, rows, pre_grad

    sent, wide, rows_two, pre_grad = lax.cond(first, stage_two_lower, stage_two_upper)
    grad_hid = swap(sent)

    def stage_three_lower():
        grads = exchange(place(grad_hid, ids, slots, prob, experts, cap))
        back, pre_grad_low = expert_backward(grads, wide, w_in, w_out, rows_one, norm_gain)
        got = exchange(back)
        first_grad, second_grad = weight_grads(rows_one, norm_gain, grads, w_in, pre_grad_low)
        return gather(got, ids, slots, None, grad_hid, cap), first_grad, second_grad

    def stage_three_upper():
        part = expert_forward(rows_two, norm_gain, w_in, w_out)
        first_grad, second_grad = weight_grads(rows_two, norm_gain, rows_one, w_in, pre_grad)
        part, first_grad, second_grad = lax.optimization_barrier((part, first_grad, second_grad))
        return gather(exchange(part), ids, slots, prob, hid, cap), first_grad, second_grad

    result, first_grad, second_grad = lax.cond(first, stage_three_lower, stage_three_upper)
    return result[None], first_grad[None, None], second_grad[None, None]


def solution(mesh):
    placed = (
        P("section", None, "expert", "head"),
        P("section", None),
        P("section", None, "expert"),
        P("section", None, "expert"),
        P("section", None, "expert"),
        P("section", "expert", None, "head"),
        P("section", "expert", "head", None),
    )
    return jax.shard_map(
        on_device,
        mesh=mesh,
        in_specs=placed,
        out_specs=(
            P("section", None, "expert", "head"),
            P("section", "expert", None, "head"),
            P("section", "expert", "head", None),
        ),
        check_vma=False,
    )
```

```python
import functools

import jax
import jax.numpy as jnp
from jax import lax
from jax.experimental import pallas as pl
from jax.experimental.pallas import tpu as pltpu
from jax.sharding import PartitionSpec as P

EPSILON = 1e-06
ROOT_COEF = 0.7978845608
CUBE_COEF = 0.044715
VMEM_LIMIT = 24 * 1024 * 1024
BF16, F32 = jnp.bfloat16, jnp.float32


def activate(v):
    sq = v * v
    th = jnp.tanh(ROOT_COEF * (v + CUBE_COEF * sq * v))
    up = 0.5 * (1.0 + th)
    return th, sq, up


def act_of(v):
    _, _, up = activate(v)
    return v * up


def act_and_slope(v):
    th, sq, up = activate(v)
    slope = up + 0.5 * v * (1.0 - th * th) * (ROOT_COEF + (3.0 * CUBE_COEF * ROOT_COEF) * sq)
    return v * up, slope


def dot(a, b, dims=((1,), (0,))):
    return lax.dot_general(a, b, (dims, ((), ())), preferred_element_type=F32)


def call(body, outs, ins, flops, grid=(), in_specs=None, out_specs=None, scratch=(), name=None):
    moved = sum(a.size * a.dtype.itemsize for a in ins)
    moved += sum(s.size * s.dtype.itemsize for s in outs)
    kwargs = {}
    if grid:
        kwargs = dict(grid=grid, in_specs=in_specs, out_specs=out_specs)
    return pl.pallas_call(
        body,
        out_shape=outs,
        scratch_shapes=scratch,
        compiler_params=pltpu.CompilerParams(vmem_limit_bytes=VMEM_LIMIT),
        cost_estimate=pl.CostEstimate(flops=flops, bytes_accessed=moved, transcendentals=0),
        name=name,
        **kwargs,
    )(*ins)


def struct(shape, dtype):
    return jax.ShapeDtypeStruct(shape, dtype)


def one_hot(ids, slots, experts, cap):
    micro, tokens = ids.shape
    per = micro * cap
    target = jnp.where(slots < cap, ids * per + slots, -1 - cap * micro)
    pieces = [target[m : m + 1] + m * cap for m in range(micro)]
    target = jnp.concatenate(pieces, axis=1)
    rows = lax.broadcasted_iota(jnp.int32, (experts * per, micro * tokens), 0)
    return (rows == target).astype(F32).astype(BF16)


def column(rows):
    flat = jnp.concatenate([rows[m : m + 1] for m in range(rows.shape[0])], axis=1)
    return jnp.transpose(jnp.broadcast_to(flat, (8, flat.shape[1])))[:, :1]


def place_body(scaled, cap, *refs):
    tok, ids, slots = refs[:3]
    outs = refs[4:] if scaled else refs[3:]
    prob = refs[3]
    experts, heads, per, _ = outs[0].shape
    tokens = tok[...].reshape(-1, tok.shape[2])
    if scaled:
        tokens = (column(prob[...]) * tokens.astype(F32)).astype(BF16)
    hot = one_hot(ids[...], slots[...], experts, cap)
    start = 0
    for out in outs:
        stop = start + out.shape[3]
        rows = dot(hot, tokens[:, start:stop]).reshape(experts, per, stop - start).astype(BF16)
        for h in range(heads):
            out[:, h] = rows
        start = stop


def place(tokens, ids, slots, prob, experts, cap, parts=None):
    micro, count, half = tokens.shape
    outs = [struct((experts, 2, micro * cap, part), BF16) for part in parts or (half,)]
    ins = (tokens, ids, slots) + (() if prob is None else (prob,))
    flops = 2 * experts * micro * cap * micro * count * half
    placed = call(functools.partial(place_body, prob is not None, cap), outs, ins, flops, name="place")
    return placed if parts else placed[0]


def gather_body(forward, cap, *refs):
    if forward:
        got, ids, slots, prob, base, out = refs
    else:
        got, ids, slots, base, out = refs
    experts, heads, per, half = got.shape
    hot = one_hot(ids[...], slots[...], experts, cap)
    first = got[:, 0].astype(F32).reshape(experts * per, half)
    second = got[:, 1].astype(F32).reshape(experts * per, half)
    if forward:
        picked = dot(hot, (first + second).astype(BF16), ((0,), (0,)))
        picked = column(prob[...]) * picked
    else:
        picked = dot(hot, first.astype(BF16), ((0,), (0,))) + dot(hot, second.astype(BF16), ((0,), (0,)))
    total = base[...].reshape(-1, half).astype(F32) + picked
    out[...] = total.astype(BF16).reshape(out.shape)


def gather(got, ids, slots, prob, base, cap):
    ins = (got, ids, slots) + (() if prob is None else (prob,)) + (base,)
    flops = 2 * got.shape[0] * got.shape[2] * base.size
    return call(
        functools.partial(gather_body, prob is not None, cap), [struct(base.shape, BF16)], ins, flops, name="gather"
    )[0]


def rows_of(ref):
    experts, heads, per, half = ref.shape
    return [ref[:, h].astype(F32).reshape(experts * per, half) for h in range(heads)]


def inverse(parts, width):
    total = sum(jnp.sum(v * v, axis=1, keepdims=True) for v in parts)
    return lax.rsqrt(total * (1.0 / width) + EPSILON)


def fill_normed(rows_ref, gain_ref, normed_ref):
    parts = rows_of(rows_ref)
    half = parts[0].shape[1]
    scale = inverse(parts, 2 * half)
    for h, v in enumerate(parts):
        cols = pl.ds(h * half, half)
        normed_ref[:, cols] = (v * scale * gain_ref[:, cols]).astype(BF16)


def spread(total, out_ref):
    experts, heads, per, half = out_ref.shape
    for h in range(heads):
        piece = total[:, h * half : (h + 1) * half]
        out_ref[:, h] = piece.reshape(experts, per, half).astype(BF16)


def spread_norm_grad(total, rows_ref, gain_ref, out_ref):
    experts, heads, per, half = out_ref.shape
    parts = rows_of(rows_ref)
    scale = inverse(parts, heads * half)
    grads = [total[:, h * half : (h + 1) * half] * gain_ref[:, pl.ds(h * half, half)] for h in range(heads)]
    cross = sum(jnp.sum(g * v, axis=1, keepdims=True) for g, v in zip(grads, parts))
    factor = scale * scale * scale * cross * (1.0 / (heads * half))
    for h in range(heads):
        piece = scale * grads[h] - parts[h] * factor
        out_ref[:, h] = piece.reshape(experts, per, half).astype(BF16)


def whole(shape):
    return pl.BlockSpec(shape, lambda j: (0,) * len(shape))


CHUNK = 256
NARROW = 128
GROUPS = 2


def sizes(rows, w_in):
    count = rows.shape[0] * rows.shape[2]
    width, hidden = w_in.shape
    return count, width, hidden


def expert_group(ref, r):
    step = ref.shape[0] // GROUPS
    return ref.at[pl.ds(r * step, step)]


def row_group(ref, r):
    step = ref.shape[0] // GROUPS
    return ref.at[pl.ds(pl.multiple_of(r * step, step), step)]


def over_groups(body):
    pl.loop(0, GROUPS)(body)


def copies_of(pairs, sems):
    return [pltpu.make_async_copy(src, dst, sems.at[i]) for i, (src, dst) in enumerate(pairs)]


def start_all(copies):
    for copy in copies:
        copy.start()


def flatten(grads, flat):
    half = grads.shape[3]
    for h, v in enumerate(rows_of(grads)):
        flat[:, pl.ds(h * half, half)] = v.astype(BF16)


def owned(body, outs, ins, flops, scratch, sems, name):
    moved = sum(a.size * a.dtype.itemsize for a in ins)
    moved += sum(s.size * s.dtype.itemsize for s in outs)
    return pl.pallas_call(
        body,
        out_shape=outs,
        in_specs=[
            pl.BlockSpec(memory_space=pltpu.VMEM if a.size < 4096 else pl.ANY) for a in ins
        ],
        out_specs=[pl.BlockSpec(memory_space=pl.ANY) for _ in outs],
        scratch_shapes=[pltpu.VMEM(shape, dtype) for shape, dtype in scratch] + [pltpu.SemaphoreType.DMA((sems,))],
        compiler_params=pltpu.CompilerParams(vmem_limit_bytes=VMEM_LIMIT),
        cost_estimate=pl.CostEstimate(flops=flops, bytes_accessed=moved, transcendentals=0),
        name=name,
    )(*ins)


def forward_body(rows, gain, w_in, w_out, out, rows_v, w_in_v, w_out_v, normed, out_v, sems):
    loads = copies_of([(rows, rows_v), (w_in, w_in_v), (w_out, w_out_v)], sems)
    start_all(loads)

    def stored(r):
        return pltpu.make_async_copy(expert_group(out_v, r), expert_group(out, r), sems.at[3 + r])

    loads[0].wait()

    @over_groups
    def _(r):
        fill_normed(expert_group(rows_v, r), gain, normed)

        @pl.when(r == 0)
        def _():
            loads[1].wait()

        act = act_of(dot(normed[...], w_in_v[...])).astype(BF16)

        @pl.when(r == 0)
        def _():
            loads[2].wait()

        spread(dot(act, w_out_v[...]), expert_group(out_v, r))
        stored(r).start()

    for r in range(GROUPS):
        stored(r).wait()


def expert_forward(rows, gain, w_in, w_out):
    count, width, hidden = sizes(rows, w_in)
    return owned(
        forward_body,
        [struct(rows.shape, BF16)],
        (rows, gain, w_in, w_out),
        4 * count * width * hidden,
        [
            (rows.shape, BF16),
            (w_in.shape, BF16),
            (w_out.shape, BF16),
            ((count // GROUPS, width), BF16),
            (rows.shape, BF16),
        ],
        3 + GROUPS,
        "expert_forward",
    )[0]


def grad_act_body(grads, w_out, out, flat):
    @pl.when(pl.program_id(0) == 0)
    def _():
        flatten(grads, flat)

    out[...] = dot(flat[...], w_out[...], ((1,), (1,)))


def grad_act_early(grads, w_out):
    hidden, width = w_out.shape
    count = grads.shape[0] * grads.shape[2]
    return call(
        grad_act_body,
        [struct((count, hidden), F32)],
        (grads, w_out),
        2 * count * width * hidden,
        grid=(hidden // NARROW,),
        in_specs=[whole(grads.shape), pl.BlockSpec((NARROW, width), lambda j: (j, 0))],
        out_specs=[pl.BlockSpec((count, NARROW), lambda j: (0, j))],
        scratch=[pltpu.VMEM((count, width), BF16)],
        name="grad_act",
    )[0]


def slope_body(rows, gain, w_in, out, normed):
    @pl.when(pl.program_id(0) == 0)
    def _():
        fill_normed(rows, gain, normed)

    out[...] = act_and_slope(dot(normed[...], w_in[...]))[1]


def slope_of_rows(rows, gain, w_in):
    count, width, hidden = sizes(rows, w_in)
    return call(
        slope_body,
        [struct((count, hidden), F32)],
        (rows, gain, w_in),
        2 * count * width * hidden,
        grid=(hidden // NARROW,),
        in_specs=[whole(rows.shape), whole(gain.shape), pl.BlockSpec((width, NARROW), lambda j: (0, j))],
        out_specs=[pl.BlockSpec((count, NARROW), lambda j: (0, j))],
        scratch=[pltpu.VMEM((count, width), BF16)],
        name="slope",
    )[0]


def both_body(rows, gain, w_in, grad_act, out, kept, rows_v, w_in_v, ga_v, normed, pre_grad, out_v, sems):
    loads = copies_of([(rows, rows_v), (w_in, w_in_v), (grad_act, ga_v)], sems)
    start_all(loads)

    def stored(r):
        return pltpu.make_async_copy(expert_group(out_v, r), expert_group(out, r), sems.at[3 + r])

    def saved(r):
        return pltpu.make_async_copy(row_group(pre_grad, r), row_group(kept, r), sems.at[3 + GROUPS + r])

    loads[0].wait()

    @over_groups
    def _(r):
        row = expert_group(rows_v, r)
        fill_normed(row, gain, normed)

        @pl.when(r == 0)
        def _():
            loads[1].wait()

        slope = act_and_slope(dot(normed[...], w_in_v[...]))[1]

        @pl.when(r == 0)
        def _():
            loads[2].wait()

        pre = (row_group(ga_v, r)[...] * slope).astype(BF16)
        row_group(pre_grad, r)[...] = pre
        saved(r).start()
        spread_norm_grad(dot(pre, w_in_v[...], ((1,), (1,))), row, gain, expert_group(out_v, r))
        stored(r).start()

    for r in range(GROUPS):
        stored(r).wait()
        saved(r).wait()


def expert_both(rows, gain, w_in, grad_act):
    count, width, hidden = sizes(rows, w_in)
    return owned(
        both_body,
        [struct(rows.shape, BF16), struct((count, hidden), BF16)],
        (rows, gain, w_in, grad_act),
        4 * count * width * hidden,
        [
            (rows.shape, BF16),
            (w_in.shape, BF16),
            ((count, hidden), F32),
            ((count // GROUPS, width), BF16),
            ((count, hidden), BF16),
            (rows.shape, BF16),
        ],
        3 + 2 * GROUPS,
        "expert_both",
    )


def backward_body(
    grads, slope, w_in, w_out, rows, gain, out, kept, grads_v, slope_v, w_in_v, w_out_v, rows_v, flat, pre_grad, out_v, sems
):
    pairs = [(grads, grads_v), (w_out, w_out_v), (slope, slope_v), (w_in, w_in_v), (rows, rows_v)]
    loads = copies_of(pairs, sems)
    start_all(loads)

    def stored(r):
        return pltpu.make_async_copy(expert_group(out_v, r), expert_group(out, r), sems.at[5 + r])

    def saved(r):
        return pltpu.make_async_copy(row_group(pre_grad, r), row_group(kept, r), sems.at[5 + GROUPS + r])

    loads[0].wait()

    for r in range(GROUPS):
        flatten(expert_group(grads_v, r), flat)

        if r == 0:
            loads[1].wait()

        grad_act = dot(flat[...], w_out_v[...], ((1,), (1,)))

        if r == 0:
            loads[2].wait()

        pre = (grad_act * row_group(slope_v, r)[...]).astype(BF16)
        row_group(pre_grad, r)[...] = pre
        saved(r).start()

        if r == 0:
            loads[3].wait()
            loads[4].wait()

        total = dot(pre, w_in_v[...], ((1,), (1,)))
        spread_norm_grad(total, expert_group(rows_v, r), gain, expert_group(out_v, r))
        stored(r).start()

    for r in range(GROUPS):
        stored(r).wait()
        saved(r).wait()


def expert_backward(grads, slope, w_in, w_out, rows, gain):
    count, width, hidden = sizes(rows, w_in)
    return owned(
        backward_body,
        [struct(rows.shape, BF16), struct((count, hidden), BF16)],
        (grads, slope, w_in, w_out, rows, gain),
        4 * count * width * hidden,
        [
            (grads.shape, BF16),
            (slope.shape, F32),
            (w_in.shape, BF16),
            (w_out.shape, BF16),
            (rows.shape, BF16),
            ((count // GROUPS, width), BF16),
            ((count, hidden), BF16),
            (rows.shape, BF16),
        ],
        5 + 2 * GROUPS,
        "expert_backward",
    )


def weight_grad_body(rows, gain, grads, w_in, pre_grad, first, second, normed, flat):
    @pl.when(pl.program_id(0) == 0)
    def _():
        fill_normed(rows, gain, normed)
        flatten(grads, flat)

    first[...] = dot(normed[...], pre_grad[...], ((0,), (0,))).astype(BF16)
    act = act_of(dot(normed[...], w_in[...])).astype(BF16)
    second[...] = dot(act, flat[...], ((0,), (0,))).astype(BF16)


def weight_grads(rows, gain, grads, w_in, pre_grad):
    count, width, hidden = sizes(rows, w_in)
    columns = pl.BlockSpec((width, CHUNK), lambda j: (0, j))
    return call(
        weight_grad_body,
        [struct((width, hidden), BF16), struct((hidden, width), BF16)],
        (rows, gain, grads, w_in, pre_grad),
        6 * count * width * hidden,
        grid=(hidden // CHUNK,),
        in_specs=[
            whole(rows.shape),
            whole(gain.shape),
            whole(grads.shape),
            columns,
            pl.BlockSpec((count, CHUNK), lambda j: (0, j)),
        ],
        out_specs=[columns, pl.BlockSpec((CHUNK, width), lambda j: (j, 0))],
        scratch=[pltpu.VMEM((count, width), BF16), pltpu.VMEM((count, width), BF16)],
        name="weight_grads",
    )


def exchange(blocks):
    experts, heads, per, part = blocks.shape
    flat = blocks.reshape(experts * heads, per, part)
    return lax.all_to_all(flat, ("expert", "head"), 0, 0, tiled=True).reshape(blocks.shape)


def swap(block):
    count = lax.axis_size("section")
    return lax.ppermute(block, "section", [(i, (i + 1) % count) for i in range(count)])


def on_device(boundary, norm_gain, gate_prob, expert_ids, slot_ids, weight_in, weight_out):
    experts = lax.axis_size("expert")
    local = boundary[0]
    micro, count, half = local.shape
    cap = 2 * count // experts
    w_in = weight_in[0, 0]
    w_out = weight_out[0, 0]
    ids, slots, prob = expert_ids[0], slot_ids[0], gate_prob[0]
    first = lax.axis_index("section") == 0

    def stage_one_lower():
        rows = exchange(place(local, ids, slots, None, experts, cap))
        part = expert_forward(rows, norm_gain, w_in, w_out)
        return gather(exchange(part), ids, slots, prob, local, cap), rows

    def stage_one_upper():
        small, large = place(local, ids, slots, prob, experts, cap, (half // 3, half - half // 3))
        small, large = lax.optimization_barrier((exchange(small), large))
        return local, jnp.concatenate([small, exchange(large)], axis=3)

    sent, rows_one = lax.cond(first, stage_one_lower, stage_one_upper)
    hid = swap(sent)

    def stage_two_lower():
        slope = slope_of_rows(rows_one, norm_gain, w_in)
        return local, slope, rows_one, jnp.zeros(slope.shape, BF16)

    def stage_two_upper():
        rows = exchange(place(hid, ids, slots, None, experts, cap))
        grad_act = grad_act_early(rows_one, w_out)
        back, pre_grad = expert_both(rows, norm_gain, w_in, grad_act)
        grad_hid = gather(exchange(back), ids, slots, None, local, cap)
        return grad_hid, grad_act, rows, pre_grad

    sent, wide, rows_two, pre_grad = lax.cond(first, stage_two_lower, stage_two_upper)
    grad_hid = swap(sent)

    def stage_three_lower():
        grads = exchange(place(grad_hid, ids, slots, prob, experts, cap))
        back, pre_grad_low = expert_backward(grads, wide, w_in, w_out, rows_one, norm_gain)
        got = exchange(back)
        first_grad, second_grad = weight_grads(rows_one, norm_gain, grads, w_in, pre_grad_low)
        return gather(got, ids, slots, None, grad_hid, cap), first_grad, second_grad

    def stage_three_upper():
        part = expert_forward(rows_two, norm_gain, w_in, w_out)
        first_grad, second_grad = weight_grads(rows_two, norm_gain, rows_one, w_in, pre_grad)
        part, first_grad, second_grad = lax.optimization_barrier((part, first_grad, second_grad))
        return gather(exchange(part), ids, slots, prob, hid, cap), first_grad, second_grad

    result, first_grad, second_grad = lax.cond(first, stage_three_lower, stage_three_upper)
    return result[None], first_grad[None, None], second_grad[None, None]


def solution(mesh):
    placed = (
        P("section", None, "expert", "head"),
        P("section", None),
        P("section", None, "expert"),
        P("section", None, "expert"),
        P("section", None, "expert"),
        P("section", "expert", None, "head"),
        P("section", "expert", "head", None),
    )
    return jax.shard_map(
        on_device,
        mesh=mesh,
        in_specs=placed,
        out_specs=(
            P("section", None, "expert", "head"),
            P("section", "expert", None, "head"),
            P("section", "expert", "head", None),
        ),
        check_vma=False,
    )
```

```python
import functools

import jax
import jax.numpy as jnp
from jax import lax
from jax.experimental import pallas as pl
from jax.experimental.pallas import tpu as pltpu
from jax.sharding import PartitionSpec as P

EPSILON = 1e-06
ROOT_COEF = 0.7978845608
CUBE_COEF = 0.044715
VMEM_LIMIT = 24 * 1024 * 1024
BF16, F32 = jnp.bfloat16, jnp.float32


def activate(v):
    sq = v * v
    th = jnp.tanh(ROOT_COEF * (v + CUBE_COEF * sq * v))
    up = 0.5 * (1.0 + th)
    return th, sq, up


def act_of(v):
    _, _, up = activate(v)
    return v * up


def act_and_slope(v):
    th, sq, up = activate(v)
    slope = up + 0.5 * v * (1.0 - th * th) * (ROOT_COEF + (3.0 * CUBE_COEF * ROOT_COEF) * sq)
    return v * up, slope


def dot(a, b, dims=((1,), (0,))):
    return lax.dot_general(a, b, (dims, ((), ())), preferred_element_type=F32)


def call(body, outs, ins, flops, grid=(), in_specs=None, out_specs=None, scratch=(), name=None):
    moved = sum(a.size * a.dtype.itemsize for a in ins)
    moved += sum(s.size * s.dtype.itemsize for s in outs)
    kwargs = {}
    if grid:
        kwargs = dict(grid=grid, in_specs=in_specs, out_specs=out_specs)
    return pl.pallas_call(
        body,
        out_shape=outs,
        scratch_shapes=scratch,
        compiler_params=pltpu.CompilerParams(vmem_limit_bytes=VMEM_LIMIT),
        cost_estimate=pl.CostEstimate(flops=flops, bytes_accessed=moved, transcendentals=0),
        name=name,
        **kwargs,
    )(*ins)


def struct(shape, dtype):
    return jax.ShapeDtypeStruct(shape, dtype)


def one_hot(ids, slots, experts, cap):
    micro, tokens = ids.shape
    per = micro * cap
    target = jnp.where(slots < cap, ids * per + slots, -1 - cap * micro)
    pieces = [target[m : m + 1] + m * cap for m in range(micro)]
    target = jnp.concatenate(pieces, axis=1)
    rows = lax.broadcasted_iota(jnp.int32, (experts * per, micro * tokens), 0)
    return (rows == target).astype(F32).astype(BF16)


def column(rows):
    flat = jnp.concatenate([rows[m : m + 1] for m in range(rows.shape[0])], axis=1)
    return jnp.transpose(jnp.broadcast_to(flat, (8, flat.shape[1])))[:, :1]


def place_body(scaled, cap, *refs):
    tok, ids, slots = refs[:3]
    outs = refs[4:] if scaled else refs[3:]
    prob = refs[3]
    experts, heads, per, _ = outs[0].shape
    tokens = tok[...].reshape(-1, tok.shape[2])
    if scaled:
        tokens = (column(prob[...]) * tokens.astype(F32)).astype(BF16)
    hot = one_hot(ids[...], slots[...], experts, cap)
    start = 0
    for out in outs:
        stop = start + out.shape[3]
        rows = dot(hot, tokens[:, start:stop]).reshape(experts, per, stop - start).astype(BF16)
        for h in range(heads):
            out[:, h] = rows
        start = stop


def place(tokens, ids, slots, prob, experts, cap, parts=None):
    micro, count, half = tokens.shape
    outs = [struct((experts, 2, micro * cap, part), BF16) for part in parts or (half,)]
    ins = (tokens, ids, slots) + (() if prob is None else (prob,))
    flops = 2 * experts * micro * cap * micro * count * half
    placed = call(functools.partial(place_body, prob is not None, cap), outs, ins, flops, name="place")
    return placed if parts else placed[0]


def gather_body(forward, cap, *refs):
    if forward:
        got, ids, slots, prob, base, out = refs
    else:
        got, ids, slots, base, out = refs
    experts, heads, per, half = got.shape
    hot = one_hot(ids[...], slots[...], experts, cap)
    first = got[:, 0].astype(F32).reshape(experts * per, half)
    second = got[:, 1].astype(F32).reshape(experts * per, half)
    if forward:
        picked = dot(hot, (first + second).astype(BF16), ((0,), (0,)))
        picked = column(prob[...]) * picked
    else:
        picked = dot(hot, first.astype(BF16), ((0,), (0,))) + dot(hot, second.astype(BF16), ((0,), (0,)))
    total = base[...].reshape(-1, half).astype(F32) + picked
    out[...] = total.astype(BF16).reshape(out.shape)


def gather(got, ids, slots, prob, base, cap):
    ins = (got, ids, slots) + (() if prob is None else (prob,)) + (base,)
    flops = 2 * got.shape[0] * got.shape[2] * base.size
    return call(
        functools.partial(gather_body, prob is not None, cap), [struct(base.shape, BF16)], ins, flops, name="gather"
    )[0]


def rows_of(ref):
    experts, heads, per, half = ref.shape
    return [ref[:, h].astype(F32).reshape(experts * per, half) for h in range(heads)]


def inverse(parts, width):
    total = sum(jnp.sum(v * v, axis=1, keepdims=True) for v in parts)
    return lax.rsqrt(total * (1.0 / width) + EPSILON)


def fill_normed(rows_ref, gain_ref, normed_ref):
    parts = rows_of(rows_ref)
    half = parts[0].shape[1]
    scale = inverse(parts, 2 * half)
    for h, v in enumerate(parts):
        cols = pl.ds(h * half, half)
        normed_ref[:, cols] = (v * scale * gain_ref[:, cols]).astype(BF16)


def spread(total, out_ref):
    experts, heads, per, half = out_ref.shape
    for h in range(heads):
        piece = total[:, h * half : (h + 1) * half]
        out_ref[:, h] = piece.reshape(experts, per, half).astype(BF16)


def spread_norm_grad(total, rows_ref, gain_ref, out_ref):
    experts, heads, per, half = out_ref.shape
    parts = rows_of(rows_ref)
    scale = inverse(parts, heads * half)
    grads = [total[:, h * half : (h + 1) * half] * gain_ref[:, pl.ds(h * half, half)] for h in range(heads)]
    cross = sum(jnp.sum(g * v, axis=1, keepdims=True) for g, v in zip(grads, parts))
    factor = scale * scale * scale * cross * (1.0 / (heads * half))
    for h in range(heads):
        piece = scale * grads[h] - parts[h] * factor
        out_ref[:, h] = piece.reshape(experts, per, half).astype(BF16)


def whole(shape):
    return pl.BlockSpec(shape, lambda j: (0,) * len(shape))


CHUNK = 128
NARROW = 128
GROUPS = 2


def sizes(rows, w_in):
    count = rows.shape[0] * rows.shape[2]
    width, hidden = w_in.shape
    return count, width, hidden


def expert_group(ref, r):
    step = ref.shape[0] // GROUPS
    return ref.at[pl.ds(r * step, step)]


def row_group(ref, r):
    step = ref.shape[0] // GROUPS
    return ref.at[pl.ds(pl.multiple_of(r * step, step), step)]


def over_groups(body):
    pl.loop(0, GROUPS)(body)


def copies_of(pairs, sems):
    return [pltpu.make_async_copy(src, dst, sems.at[i]) for i, (src, dst) in enumerate(pairs)]


def start_all(copies):
    for copy in copies:
        copy.start()


def flatten(grads, flat):
    half = grads.shape[3]
    for h, v in enumerate(rows_of(grads)):
        flat[:, pl.ds(h * half, half)] = v.astype(BF16)


def owned(body, outs, ins, flops, scratch, sems, name):
    moved = sum(a.size * a.dtype.itemsize for a in ins)
    moved += sum(s.size * s.dtype.itemsize for s in outs)
    return pl.pallas_call(
        body,
        out_shape=outs,
        in_specs=[
            pl.BlockSpec(memory_space=pltpu.VMEM if a.size < 4096 else pl.ANY) for a in ins
        ],
        out_specs=[pl.BlockSpec(memory_space=pl.ANY) for _ in outs],
        scratch_shapes=[pltpu.VMEM(shape, dtype) for shape, dtype in scratch] + [pltpu.SemaphoreType.DMA((sems,))],
        compiler_params=pltpu.CompilerParams(vmem_limit_bytes=VMEM_LIMIT),
        cost_estimate=pl.CostEstimate(flops=flops, bytes_accessed=moved, transcendentals=0),
        name=name,
    )(*ins)


def forward_body(rows, gain, w_in, w_out, out, kept, rows_v, w_in_v, w_out_v, normed, out_v, pre_v, sems):
    loads = copies_of([(rows, rows_v), (w_in, w_in_v), (w_out, w_out_v)], sems)
    start_all(loads)

    def stored(r):
        return pltpu.make_async_copy(expert_group(out_v, r), expert_group(out, r), sems.at[3 + r])

    def saved(r):
        return pltpu.make_async_copy(row_group(pre_v, r), row_group(kept, r), sems.at[3 + GROUPS + r])

    loads[0].wait()

    @over_groups
    def _(r):
        fill_normed(expert_group(rows_v, r), gain, normed)

        @pl.when(r == 0)
        def _():
            loads[1].wait()

        pre = dot(normed[...], w_in_v[...])
        row_group(pre_v, r)[...] = pre
        saved(r).start()
        act = act_of(pre).astype(BF16)

        @pl.when(r == 0)
        def _():
            loads[2].wait()

        spread(dot(act, w_out_v[...]), expert_group(out_v, r))
        stored(r).start()

    for r in range(GROUPS):
        stored(r).wait()
        saved(r).wait()


def expert_forward(rows, gain, w_in, w_out):
    count, width, hidden = sizes(rows, w_in)
    return owned(
        forward_body,
        [struct(rows.shape, BF16), struct((count, hidden), F32)],
        (rows, gain, w_in, w_out),
        4 * count * width * hidden,
        [
            (rows.shape, BF16),
            (w_in.shape, BF16),
            (w_out.shape, BF16),
            ((count // GROUPS, width), BF16),
            (rows.shape, BF16),
            ((count, hidden), F32),
        ],
        3 + 2 * GROUPS,
        "expert_forward",
    )


def grad_act_body(grads, w_out, out, flat):
    @pl.when(pl.program_id(0) == 0)
    def _():
        flatten(grads, flat)

    out[...] = dot(flat[...], w_out[...], ((1,), (1,)))


def grad_act_early(grads, w_out):
    hidden, width = w_out.shape
    count = grads.shape[0] * grads.shape[2]
    return call(
        grad_act_body,
        [struct((count, hidden), F32)],
        (grads, w_out),
        2 * count * width * hidden,
        grid=(hidden // NARROW,),
        in_specs=[whole(grads.shape), pl.BlockSpec((NARROW, width), lambda j: (j, 0))],
        out_specs=[pl.BlockSpec((count, NARROW), lambda j: (0, j))],
        scratch=[pltpu.VMEM((count, width), BF16)],
        name="grad_act",
    )[0]


def slope_body(pre, out):
    out[...] = act_and_slope(pre[...])[1]


def slope_of(pre):
    count, hidden = pre.shape
    block = pl.BlockSpec((NARROW, NARROW), lambda i, j: (i, j))
    return call(
        slope_body,
        [struct(pre.shape, F32)],
        (pre,),
        20 * count * hidden,
        grid=(count // NARROW, hidden // NARROW),
        in_specs=[block],
        out_specs=[block],
        name="slope",
    )[0]


def both_body(rows, gain, w_in, grad_act, out, kept, rows_v, w_in_v, ga_v, normed, pre_grad, out_v, sems):
    loads = copies_of([(rows, rows_v), (w_in, w_in_v)], sems)
    start_all(loads)

    def wide(r):
        return pltpu.make_async_copy(row_group(grad_act, r), row_group(ga_v, r), sems.at[2 + r])

    def stored(r):
        return pltpu.make_async_copy(expert_group(out_v, r), expert_group(out, r), sems.at[2 + GROUPS + r])

    def saved(r):
        return pltpu.make_async_copy(row_group(pre_grad, r), row_group(kept, r), sems.at[2 + 2 * GROUPS + r])

    loads[0].wait()

    @over_groups
    def _(r):
        row = expert_group(rows_v, r)
        fill_normed(row, gain, normed)

        @pl.when(r == 0)
        def _():
            loads[1].wait()
            for g in range(GROUPS):
                wide(g).start()

        slope = act_and_slope(dot(normed[...], w_in_v[...]))[1]

        wide(r).wait()
        pre = (row_group(ga_v, r)[...] * slope).astype(BF16)
        row_group(pre_grad, r)[...] = pre
        saved(r).start()
        spread_norm_grad(dot(pre, w_in_v[...], ((1,), (1,))), row, gain, expert_group(out_v, r))
        stored(r).start()

    for r in range(GROUPS):
        stored(r).wait()
        saved(r).wait()


def expert_both(rows, gain, w_in, grad_act):
    count, width, hidden = sizes(rows, w_in)
    return owned(
        both_body,
        [struct(rows.shape, BF16), struct((count, hidden), BF16)],
        (rows, gain, w_in, grad_act),
        4 * count * width * hidden,
        [
            (rows.shape, BF16),
            (w_in.shape, BF16),
            ((count, hidden), F32),
            ((count // GROUPS, width), BF16),
            ((count, hidden), BF16),
            (rows.shape, BF16),
        ],
        2 + 3 * GROUPS,
        "expert_both",
    )


def backward_body(
    grads, slope, w_in, w_out, rows, gain, out, kept, grads_v, slope_v, w_in_v, w_out_v, rows_v, flat, pre_grad, out_v, sems
):
    pairs = [(grads, grads_v), (w_out, w_out_v), (slope, slope_v), (w_in, w_in_v), (rows, rows_v)]
    loads = copies_of(pairs, sems)
    start_all(loads)

    def stored(r):
        return pltpu.make_async_copy(expert_group(out_v, r), expert_group(out, r), sems.at[5 + r])

    def saved(r):
        return pltpu.make_async_copy(row_group(pre_grad, r), row_group(kept, r), sems.at[5 + GROUPS + r])

    loads[0].wait()

    for r in range(GROUPS):
        flatten(expert_group(grads_v, r), flat)

        if r == 0:
            loads[1].wait()

        grad_act = dot(flat[...], w_out_v[...], ((1,), (1,)))

        if r == 0:
            loads[2].wait()

        pre = (grad_act * row_group(slope_v, r)[...]).astype(BF16)
        row_group(pre_grad, r)[...] = pre
        saved(r).start()

        if r == 0:
            loads[3].wait()
            loads[4].wait()

        total = dot(pre, w_in_v[...], ((1,), (1,)))
        spread_norm_grad(total, expert_group(rows_v, r), gain, expert_group(out_v, r))
        stored(r).start()

    for r in range(GROUPS):
        stored(r).wait()
        saved(r).wait()


def expert_backward(grads, slope, w_in, w_out, rows, gain):
    count, width, hidden = sizes(rows, w_in)
    return owned(
        backward_body,
        [struct(rows.shape, BF16), struct((count, hidden), BF16)],
        (grads, slope, w_in, w_out, rows, gain),
        4 * count * width * hidden,
        [
            (grads.shape, BF16),
            (slope.shape, F32),
            (w_in.shape, BF16),
            (w_out.shape, BF16),
            (rows.shape, BF16),
            ((count // GROUPS, width), BF16),
            ((count, hidden), BF16),
            (rows.shape, BF16),
        ],
        5 + 2 * GROUPS,
        "expert_backward",
    )


def weight_grad_body(rows, gain, grads, w_in, pre_grad, first, second, normed, flat):
    @pl.when(pl.program_id(0) == 0)
    def _():
        fill_normed(rows, gain, normed)
        flatten(grads, flat)

    first[...] = dot(normed[...], pre_grad[...], ((0,), (0,))).astype(BF16)
    act = act_of(dot(normed[...], w_in[...])).astype(BF16)
    second[...] = dot(act, flat[...], ((0,), (0,))).astype(BF16)


def weight_grads(rows, gain, grads, w_in, pre_grad):
    count, width, hidden = sizes(rows, w_in)
    columns = pl.BlockSpec((width, CHUNK), lambda j: (0, j))
    return call(
        weight_grad_body,
        [struct((width, hidden), BF16), struct((hidden, width), BF16)],
        (rows, gain, grads, w_in, pre_grad),
        6 * count * width * hidden,
        grid=(hidden // CHUNK,),
        in_specs=[
            whole(rows.shape),
            whole(gain.shape),
            whole(grads.shape),
            columns,
            pl.BlockSpec((count, CHUNK), lambda j: (0, j)),
        ],
        out_specs=[columns, pl.BlockSpec((CHUNK, width), lambda j: (j, 0))],
        scratch=[pltpu.VMEM((count, width), BF16), pltpu.VMEM((count, width), BF16)],
        name="weight_grads",
    )


def exchange(blocks):
    experts, heads, per, part = blocks.shape
    flat = blocks.reshape(experts * heads, per, part)
    return lax.all_to_all(flat, ("expert", "head"), 0, 0, tiled=True).reshape(blocks.shape)


def swap(block):
    count = lax.axis_size("section")
    return lax.ppermute(block, "section", [(i, (i + 1) % count) for i in range(count)])


def on_device(boundary, norm_gain, gate_prob, expert_ids, slot_ids, weight_in, weight_out):
    experts = lax.axis_size("expert")
    local = boundary[0]
    micro, count, half = local.shape
    cap = 2 * count // experts
    w_in = weight_in[0, 0]
    w_out = weight_out[0, 0]
    ids, slots, prob = expert_ids[0], slot_ids[0], gate_prob[0]
    first = lax.axis_index("section") == 0

    def stage_one_lower():
        rows = exchange(place(local, ids, slots, None, experts, cap))
        part, pre = expert_forward(rows, norm_gain, w_in, w_out)
        return gather(exchange(part), ids, slots, prob, local, cap), rows, pre

    def stage_one_upper():
        small, large = place(local, ids, slots, prob, experts, cap, (half // 3, half - half // 3))
        small, large = lax.optimization_barrier((exchange(small), large))
        grads = jnp.concatenate([small, exchange(large)], axis=3)
        return local, grads, grad_act_early(grads, w_out)

    sent, rows_one, wide_one = lax.cond(first, stage_one_lower, stage_one_upper)
    hid = swap(sent)

    def stage_two_lower():
        slope = slope_of(wide_one)
        return local, slope, rows_one, jnp.zeros(slope.shape, BF16)

    def stage_two_upper():
        rows = exchange(place(hid, ids, slots, None, experts, cap))
        back, pre_grad = expert_both(rows, norm_gain, w_in, wide_one)
        grad_hid = gather(exchange(back), ids, slots, None, local, cap)
        return grad_hid, wide_one, rows, pre_grad

    sent, wide, rows_two, pre_grad = lax.cond(first, stage_two_lower, stage_two_upper)
    grad_hid = swap(sent)

    def stage_three_lower():
        grads = exchange(place(grad_hid, ids, slots, prob, experts, cap))
        back, pre_grad_low = expert_backward(grads, wide, w_in, w_out, rows_one, norm_gain)
        got = exchange(back)
        first_grad, second_grad = weight_grads(rows_one, norm_gain, grads, w_in, pre_grad_low)
        return gather(got, ids, slots, None, grad_hid, cap), first_grad, second_grad

    def stage_three_upper():
        part = expert_forward(rows_two, norm_gain, w_in, w_out)[0]
        first_grad, second_grad = weight_grads(rows_two, norm_gain, rows_one, w_in, pre_grad)
        part, first_grad, second_grad = lax.optimization_barrier((part, first_grad, second_grad))
        return gather(exchange(part), ids, slots, prob, hid, cap), first_grad, second_grad

    result, first_grad, second_grad = lax.cond(first, stage_three_lower, stage_three_upper)
    return result[None], first_grad[None, None], second_grad[None, None]


def solution(mesh):
    placed = (
        P("section", None, "expert", "head"),
        P("section", None),
        P("section", None, "expert"),
        P("section", None, "expert"),
        P("section", None, "expert"),
        P("section", "expert", None, "head"),
        P("section", "expert", "head", None),
    )
    return jax.shard_map(
        on_device,
        mesh=mesh,
        in_specs=placed,
        out_specs=(
            P("section", None, "expert", "head"),
            P("section", "expert", None, "head"),
            P("section", "expert", "head", None),
        ),
        check_vma=False,
    )
```
